256 devices in a mesh: ctx: 32 (over z, x), head: 8 (over y, core).
Axes of the slice: x: 4, y: 4, z: 8, core: 2. Of those that a mesh axis runs over, the one named last changes fastest.
Arguments:
- query_rows: bfloat16 [98304, 4096], P('ctx', 'head'), may hold values from -6 to 6
- key_rows: bfloat16 [98304, 4096], P('ctx', 'head'), may hold values from -6 to 6
- value_rows: bfloat16 [98304, 4096], P('ctx', 'head'), may hold values from -220 to 220
- out_gain: bfloat16 [4096], P('head'), may hold values from 0.5 to 1.5
- doc_starts: int32 [16], replicated, may hold values from 0 to 98303, as said below
Outputs:
- normed: bfloat16 [98304, 4096], P('ctx', 'head')
The draws below stay inside these ranges and needn't reach their ends.
Inputs may be any that keep to these rules, and one draw needn't show every extreme that they name: `doc_starts`: ascending and distinct, the first entry 0, the last entry 98303.
All inputs are finite; a program needn't handle non-finite values.
Results may differ from the reference program's by a relative error of at most 0.001.
Values sent between devices are 32-bit elements; how exact they have to be, the bound alone decides.
A program may use at most 128 MiB of HBM per device.

```python
import math
import jax
import jax.numpy as jnp
from jax import lax

HEADS = 32
HD = 128
D = 4096
TOKENS = 98304
BLOCK = 512
NDOCS = 16


def draw_value_rows(key, part):
    first, second, third = jax.random.split(jax.random.fold_in(key, 11), 3)
    basic = jnp.clip(jax.random.normal(first, (TOKENS, HEADS, HD), jnp.float32), -6.0, 6.0)
    token_scale = jnp.exp(jax.random.uniform(third, (TOKENS,), jnp.float32, 0.0, math.log(10.0)))
    rising = math.log(3.0) * jnp.arange(HEADS, dtype=jnp.float32) / max(HEADS - 1, 1)
    head_scale = jnp.exp(rising + jax.random.uniform(second, (HEADS,), jnp.float32, 0.0, math.log(3.4)))
    scaled = basic * head_scale[None, :, None] * token_scale[:, None, None] * 0.3
    scaled = jnp.clip(scaled, -220.0, 220.0)
    return scaled.reshape(TOKENS, HEADS * HD).astype(jnp.bfloat16)


def draw_doc_starts(key, part):
    chosen = jax.random.permutation(jax.random.fold_in(key, 23), TOKENS - 2)[:NDOCS - 2] + 1
    ordered = jnp.sort(chosen.astype(jnp.int32))
    first_start = jnp.zeros((1,), jnp.int32)
    last_start = jnp.full((1,), TOKENS - 1, jnp.int32)
    return jnp.concatenate([first_start, ordered, last_start]).astype(jnp.int32)


def shard_levels(key, dims, cuts, least, top_value):
    loudness, own = 1.0, jax.random.fold_in(key, 6)
    for position, shards_of in cuts:
        draws = jnp.exp(jax.random.uniform(jax.random.fold_in(own, position), (shards_of,), jnp.float32, least / len(cuts), top_value / len(cuts)))
        loudness = loudness * jnp.repeat(draws, dims[position] // shards_of).reshape([-1 if axis == position else 1 for axis in range(len(dims))])
    return loudness


def centred(rng, extent, spread, most, cuts=(), held_as=jnp.bfloat16):
    values = jax.random.normal(rng, extent, jnp.float32) * spread
    if len(cuts) > 0:
        values = shard_levels(rng, extent, cuts, -0.22, 0.18) * values
    return jnp.clip(values, min=-most, max=most).astype(held_as)


def setup_inputs(seed: int = 0) -> dict:
    keys = jax.random.split(jax.random.key(seed), 6)
    query_rows = centred(keys[0], (TOKENS, D), 1.0, 6.0, ((0, 32), (1, 8)))
    key_rows = centred(keys[1], (TOKENS, D), 1.0, 6.0, ((0, 32), (1, 8)))
    value_rows = draw_value_rows(jax.random.fold_in(keys[5], 71), 0)
    out_gain = jnp.clip(1.0 + 0.1 * jax.random.normal(keys[3], (D,), jnp.float32), 0.5, 1.5).astype(jnp.bfloat16)
    doc_starts = draw_doc_starts(jax.random.fold_in(keys[5], 71), 0)
    return {"query_rows": query_rows, "key_rows": key_rows, "value_rows": value_rows, "out_gain": out_gain, "doc_starts": doc_starts}


def segment_of(positions, doc_starts):
    return lax.optimization_barrier(jnp.sum((doc_starts <= positions[..., None]).astype(jnp.int32), axis=-1)) - 1

def reference(query_rows, key_rows, value_rows, out_gain, doc_starts):
    tokens = query_rows.shape[0]
    block_count = tokens // BLOCK
    queries = query_rows.reshape(block_count, BLOCK, HEADS, HD)
    keyset = key_rows.reshape(block_count, BLOCK, HEADS, HD)
    valueset = value_rows.reshape(block_count, BLOCK, HEADS, HD)
    positions = jnp.arange(tokens, dtype=jnp.int32).reshape(block_count, BLOCK)
    segment = segment_of(positions, doc_starts)
    before = segment_of(positions[:, 0] - 1, doc_starts)
    causal = jnp.arange(BLOCK)[:, None] >= jnp.arange(BLOCK)[None, :]
    highest = lax.Precision.HIGHEST

    def advance(carried, items):
        query_blk, key_blk, value_blk, seg_blk, seg_before = items
        query_f = query_blk.astype(jnp.float32)
        key_f = key_blk.astype(jnp.float32)
        value_f = value_blk.astype(jnp.float32)
        scores = jnp.einsum('ihd,jhd->hij', query_f, key_f, precision=highest)
        allowed = causal & (seg_blk[:, None] == seg_blk[None, :])
        scores = jnp.where(allowed[None], scores, jnp.float32(0.0))
        within = jnp.einsum('hij,jhe->ihe', scores, value_f, precision=highest)
        across = jnp.einsum('ihd,hde->ihe', query_f, carried, precision=highest)
        live = (seg_blk == seg_before)[:, None, None]
        result = within + jnp.where(live, across, jnp.float32(0.0))
        tail_mask = (seg_blk == seg_blk[-1])[:, None, None]
        masked_keys = jnp.where(tail_mask, key_f, jnp.float32(0.0))
        contrib = jnp.einsum('ihd,ihe->hde', masked_keys, value_f, precision=highest)
        reset = seg_blk[-1] != seg_before
        carried = jnp.where(reset, contrib, carried + contrib)
        return (carried, result)
    initial = jnp.zeros((HEADS, HD, HD), jnp.float32)
    _, attended = lax.scan(advance, initial, (queries, keyset, valueset, segment, before))
    attended = attended.reshape(tokens, HEADS * HD)
    squares = lax.optimization_barrier(jnp.sum(attended * attended, axis=1, keepdims=True))
    normed = attended * lax.rsqrt(squares / (HEADS * HD) + 1e-06) * out_gain.astype(jnp.float32)[None, :]
    return normed.astype(jnp.bfloat16)
```

```python
import functools

import jax
import jax.numpy as jnp
from jax import lax
from jax.experimental import pallas as pl
from jax.experimental.pallas import tpu as pltpu
from jax.sharding import PartitionSpec as P

HEADS = 32
HD = 128
CHUNK = 128
GROUP = 1024
PIECE = 16
NZ, NX = 8, 4
SPLIT = 12
MESH = pl.DeviceIdType.MESH


def offsets():
    def hops(offset):
        return min(offset[0], NZ - offset[0]) + min(offset[1], NX - offset[1])

    pairs = [(dz, dx) for dz in range(NZ) for dx in range(NX) if dz or dx]
    return sorted(pairs, key=hops, reverse=True)


def send(src, dst, send_sem, recv_sem, device):
    pltpu.make_async_remote_copy(
        src_ref=src,
        dst_ref=dst,
        send_sem=send_sem,
        recv_sem=recv_sem,
        device_id=device,
        device_id_type=MESH,
    ).start()


def wait_bytes(ref, sem):
    pltpu.make_async_copy(ref, ref, sem).wait()


def halves(x):
    high = x.astype(jnp.bfloat16)
    return high, (x - high.astype(jnp.float32)).astype(jnp.bfloat16)


def kernel(
    starts,
    q_hbm,
    k_hbm,
    v_hbm,
    gain_ref,
    out_hbm,
    q_ref,
    k_ref,
    v_ref,
    att,
    out_ref,
    state,
    summ,
    gath,
    sums,
    incoming,
    squares,
    squares_in,
    load_sem,
    store_sem,
    ctx_send,
    ctx_recv,
    head_send,
    head_recv,
):
    rows = q_ref.shape[0]
    head_count = q_ref.shape[1] // HD
    groups = rows // GROUP
    blocks = GROUP // 128
    docs = starts.shape[0]
    peers = NZ * NX
    teams = lax.axis_size("head")

    loads = []
    for g in range(groups):
        part = pl.ds(g * GROUP, GROUP)
        loads.append(pltpu.make_async_copy(k_hbm.at[part], k_ref.at[part], load_sem.at[0, g]))
        loads.append(pltpu.make_async_copy(v_hbm.at[part], v_ref.at[part], load_sem.at[1, g]))
    for g in range(groups):
        part = pl.ds(g * GROUP, GROUP)
        loads.append(pltpu.make_async_copy(q_hbm.at[part], q_ref.at[part], load_sem.at[2, g]))
    for load in loads:
        load.start()

    me = lax.axis_index("ctx")
    team = lax.axis_index("head")
    z, x = me // NX, me % NX
    owners = [lax.rem(z + dz, NZ) * NX + lax.rem(x + dx, NX) for dz, dx in offsets()]
    mates = [lax.rem(team + d, teams) for d in (4, 5, 3, 2, 6, 1, 7)]
    barrier = pltpu.get_barrier_semaphore()
    for t in owners:
        pl.semaphore_signal(barrier, inc=1, device_id={"ctx": t}, device_id_type=MESH)
    for t in mates:
        pl.semaphore_signal(barrier, inc=1, device_id={"head": t}, device_id_type=MESH)

    anchor = me * rows
    start = [starts[d] for d in range(docs)]

    def last_start(position):
        last = start[0]
        for d in range(1, docs):
            last = jnp.where(start[d] <= position, start[d], last)
        return last

    def first_start(position):
        first = jnp.int32(2**30)
        for d in range(docs - 1, -1, -1):
            first = jnp.where(start[d] >= position, start[d], first)
        return first

    tail = last_start(anchor + rows - 1) - anchor
    row = lax.broadcasted_iota(jnp.int32, (GROUP, HD), 0)
    for g in range(groups):
        loads[2 * g].wait()
        loads[2 * g + 1].wait()
        part = pl.ds(g * GROUP, GROUP)
        keep = jnp.where(row + g * GROUP >= tail, 1.0, 0.0).astype(jnp.bfloat16)
        for h in range(head_count):
            lanes = pl.ds(h * HD, HD)
            add = lax.dot_general(
                k_ref[part, lanes] * keep,
                v_ref[part, lanes],
                (((0,), (0,)), ((), ())),
                preferred_element_type=jnp.float32,
            ).reshape(NZ, PIECE, HD)
            summ[:, h] = add if g == 0 else summ[:, h] + add

    pl.semaphore_wait(barrier, peers - 1 + teams - 1)
    for (dz, dx), t in zip(offsets(), owners):
        tz, tx = lax.rem(z + dz, NZ), lax.rem(x + dx, NX)
        send(summ.at[tz, tx], gath.at[me], ctx_send.at[0], ctx_recv.at[0], {"ctx": t})
    gath[me] = summ[z, x]

    for g in range(groups):
        loads[2 * groups + g].wait()
    state[...] = jnp.zeros_like(state)

    def local(c, _):
        r0 = pl.multiple_of(c * CHUNK, CHUNK)
        part = pl.ds(r0, CHUNK)
        base = anchor + r0
        position = base + lax.broadcasted_iota(jnp.int32, (CHUNK, HD), 0)
        source = base + lax.broadcasted_iota(jnp.int32, (CHUNK, CHUNK), 1)
        since = jnp.full((CHUNK, HD), start[0], jnp.int32)
        for d in range(1, docs):
            since = jnp.where(position >= start[d], start[d], since)
        allowed = (source <= position) & (source >= since)
        final = last_start(base + CHUNK - 1)
        live = jnp.where(position < first_start(base), 1.0, 0.0).astype(jnp.bfloat16)
        keep = jnp.where(position >= final, 1.0, 0.0).astype(jnp.bfloat16)
        carry_on = jnp.where(final >= base, 0.0, 1.0)
        for h in range(head_count):
            lanes = pl.ds(h * HD, HD)
            q, k, v = q_ref[part, lanes], k_ref[part, lanes], v_ref[part, lanes]
            scores = lax.dot_general(
                q, k, (((1,), (1,)), ((), ())), preferred_element_type=jnp.float32
            )
            s_high, s_low = halves(jnp.where(allowed, scores, 0.0))
            before = state[h]
            b_high, b_low = halves(before)
            q_live = q * live
            within = jnp.dot(
                jnp.concatenate([s_high, s_low], axis=1),
                jnp.concatenate([v, v], axis=0),
                preferred_element_type=jnp.float32,
            )
            across = jnp.dot(
                jnp.concatenate([q_live, q_live], axis=1),
                jnp.concatenate([b_high, b_low], axis=0),
                preferred_element_type=jnp.float32,
            )
            att[part, lanes] = within + across
            contrib = lax.dot_general(
                k * keep, v, (((0,), (0,)), ((), ())), preferred_element_type=jnp.float32
            )
            state[h] = before * carry_on + contrib
        return 0

    lax.fori_loop(0, SPLIT, local, 0)

    slab = lax.broadcasted_iota(jnp.int32, (peers, HD), 0)
    since = jnp.full((peers, HD), start[0], jnp.int32)
    for d in range(1, docs):
        since = jnp.where((slab + 1) * rows - 1 >= start[d], start[d], since)
    going_on = jnp.where(since >= slab * rows, 0.0, 1.0)
    wait_bytes(gath.at[pl.ds(0, peers - 1)], ctx_recv.at[0])
    carry = jnp.zeros((PIECE, HD), jnp.float32)
    for m in range(peers):
        sums[m] = carry
        carry = carry * going_on[m : m + 1] + gath[m]
    for t in owners:
        send(sums.at[t], incoming.at[me], ctx_send.at[1], ctx_recv.at[1], {"ctx": t})
    incoming[me] = sums[me]

    lax.fori_loop(SPLIT, rows // CHUNK, local, 0)

    wait_bytes(incoming.at[pl.ds(0, peers - 1)], ctx_recv.at[1])
    entry = first_start(anchor) - anchor
    entering = []
    for h in range(head_count):
        whole = jnp.concatenate([incoming[s * NX + h] for s in range(NZ)], axis=0)
        entering.append(jnp.concatenate(halves(whole), axis=0))
    eye = lax.broadcasted_iota(jnp.int32, (128, 128), 0) == lax.broadcasted_iota(
        jnp.int32, (128, 128), 1
    )
    for g in range(groups):

        def finish(b, _, g=g):
            r0 = pl.multiple_of(g * GROUP + b * 128, 128)
            part = pl.ds(r0, 128)
            position = r0 + lax.broadcasted_iota(jnp.int32, (128, HD), 0)
            live = jnp.where(position < entry, 1.0, 0.0).astype(jnp.bfloat16)
            total = jnp.zeros((128, HD), jnp.float32)
            for h in range(head_count):
                lanes = pl.ds(h * HD, HD)
                q = q_ref[part, lanes] * live
                a = att[part, lanes] + jnp.dot(
                    jnp.concatenate([q, q], axis=1),
                    entering[h],
                    preferred_element_type=jnp.float32,
                )
                att[part, lanes] = a
                total = total + a * a
            column = jnp.sum(total, axis=1, keepdims=True)
            squares[g, pl.ds(b, 1)] = jnp.sum(
                jnp.where(eye, column, 0.0), axis=0, keepdims=True
            )
            return 0

        lax.fori_loop(0, blocks, finish, 0)
        for t in mates:
            send(
                squares.at[g], squares_in.at[g, team], head_send.at[g], head_recv.at[g], {"head": t}
            )
        squares_in[g, team] = squares[g]

    gain = gain_ref[...].astype(jnp.float32)
    stores = []
    for g in range(groups):
        wait_bytes(squares_in.at[g, pl.ds(0, teams - 1)], head_recv.at[g])
        total = squares_in[g, 0]
        for m in range(1, teams):
            total = total + squares_in[g, m]
        scale = lax.rsqrt(total / (HEADS * HD) + 1e-06)
        for b in range(blocks):
            part = pl.ds(g * GROUP + b * 128, 128)
            column = jnp.sum(jnp.where(eye, scale[b : b + 1], 0.0), axis=1, keepdims=True)
            out_ref[part] = (att[part] * column * gain).astype(jnp.bfloat16)
        part = pl.ds(g * GROUP, GROUP)
        store = pltpu.make_async_copy(out_ref.at[part], out_hbm.at[part], store_sem.at[g])
        store.start()
        stores.append(store)

    for store in stores:
        store.wait()
    for side in range(2):
        wait_bytes((gath, incoming)[side].at[pl.ds(0, peers - 1)], ctx_send.at[side])
    for g in range(groups):
        wait_bytes(squares_in.at[g, pl.ds(0, teams - 1)], head_send.at[g])


def shards(query_rows, key_rows, value_rows, out_gain, doc_starts):
    rows, features = query_rows.shape
    head_count = features // HD
    groups = rows // GROUP
    peers = lax.axis_size("ctx")
    teams = lax.axis_size("head")
    smem = pl.BlockSpec(memory_space=pltpu.SMEM)
    hbm = pl.BlockSpec(memory_space=pl.ANY)
    vmem = pl.BlockSpec(memory_space=pltpu.VMEM)
    f32 = jnp.float32
    dma = pltpu.SemaphoreType.DMA
    return pl.pallas_call(
        kernel,
        out_shape=jax.ShapeDtypeStruct((rows, features), jnp.bfloat16),
        in_specs=[smem, hbm, hbm, hbm, vmem],
        out_specs=hbm,
        scratch_shapes=[
            pltpu.VMEM((rows, features), jnp.bfloat16),
            pltpu.VMEM((rows, features), jnp.bfloat16),
            pltpu.VMEM((rows, features), jnp.bfloat16),
            pltpu.VMEM((rows, features), f32),
            pltpu.VMEM((rows, features), jnp.bfloat16),
            pltpu.VMEM((head_count, HD, HD), f32),
            pltpu.VMEM((NZ, NX, PIECE, HD), f32),
            pltpu.VMEM((peers, PIECE, HD), f32),
            pltpu.VMEM((peers, PIECE, HD), f32),
            pltpu.VMEM((peers, PIECE, HD), f32),
            pltpu.VMEM((groups, GROUP // 128, 128), f32),
            pltpu.VMEM((groups, teams, GROUP // 128, 128), f32),
            dma((3, groups)),
            dma((groups,)),
            dma((2,)),
            dma((2,)),
            dma((groups,)),
            dma((groups,)),
        ],
        compiler_params=pltpu.CompilerParams(
            collective_id=0, has_side_effects=True, vmem_limit_bytes=48 * 2**20
        ),
    )(doc_starts, query_rows, key_rows, value_rows, out_gain.reshape(1, features))


def solution(mesh):
    placed = (P("ctx", "head"), P("ctx", "head"), P("ctx", "head"), P("head"), P())
    return jax.shard_map(
        shards, mesh=mesh, in_specs=placed, out_specs=P("ctx", "head"), check_vma=False
    )
```

```python
import functools

import jax
import jax.numpy as jnp
from jax import lax
from jax.experimental import pallas as pl
from jax.experimental.pallas import tpu as pltpu
from jax.sharding import PartitionSpec as P

HEADS = 32
HD = 128
CHUNK = 128
GROUP = 1024
PIECE = 16
NZ, NX = 8, 4
SPLIT = 12
FINAL = 512
MESH = pl.DeviceIdType.MESH


def offsets():
    def hops(offset):
        return min(offset[0], NZ - offset[0]) + min(offset[1], NX - offset[1])

    pairs = [(dz, dx) for dz in range(NZ) for dx in range(NX) if dz or dx]
    return sorted(pairs, key=hops, reverse=True)


def send(src, dst, send_sem, recv_sem, device):
    pltpu.make_async_remote_copy(
        src_ref=src,
        dst_ref=dst,
        send_sem=send_sem,
        recv_sem=recv_sem,
        device_id=device,
        device_id_type=MESH,
    ).start()


def wait_bytes(ref, sem):
    pltpu.make_async_copy(ref, ref, sem).wait()


def halves(x):
    high = x.astype(jnp.bfloat16)
    return high, (x - high.astype(jnp.float32)).astype(jnp.bfloat16)


def diagonal(first, second):
    zeros = jnp.zeros_like(first)
    return jnp.concatenate(
        [jnp.concatenate([first, zeros], axis=1), jnp.concatenate([zeros, second], axis=1)], axis=0
    )


def apart(pair):
    return diagonal(pair[:, :HD], pair[:, HD:])


def dot(a, b):
    return jnp.dot(a, b, preferred_element_type=jnp.float32)


def kernel(
    starts_hbm,
    q_hbm,
    k_hbm,
    v_hbm,
    gain_hbm,
    out_ref,
    starts,
    gain_ref,
    q_ref,
    k_ref,
    v_ref,
    att,
    state,
    summ,
    gath,
    sums,
    incoming,
    squares,
    squares_in,
    load_sem,
    small_sem,
    ctx_send,
    ctx_recv,
    head_send,
    head_recv,
):
    rows = q_ref.shape[0]
    head_count = q_ref.shape[1] // HD
    groups = rows // GROUP
    blocks = GROUP // 128
    docs = starts.shape[0]
    peers = NZ * NX
    teams = lax.axis_size("head")

    me = lax.axis_index("ctx")
    team = lax.axis_index("head")
    z, x = me // NX, me % NX
    owners = [lax.rem(z + dz, NZ) * NX + lax.rem(x + dx, NX) for dz, dx in offsets()]
    mates = [lax.rem(team + d, teams) for d in (4, 5, 3, 2, 6, 1, 7)]
    barrier = pltpu.get_barrier_semaphore()
    for t in owners:
        pl.semaphore_signal(barrier, inc=1, device_id={"ctx": t}, device_id_type=MESH)
    for t in mates:
        pl.semaphore_signal(barrier, inc=1, device_id={"head": t}, device_id_type=MESH)

    small = [
        pltpu.make_async_copy(starts_hbm, starts, small_sem.at[0]),
        pltpu.make_async_copy(gain_hbm, gain_ref, small_sem.at[1]),
    ]
    loads = []
    for g in range(groups):
        part = pl.ds(g * GROUP, GROUP)
        loads.append(pltpu.make_async_copy(k_hbm.at[part], k_ref.at[part], load_sem.at[0, g]))
        loads.append(pltpu.make_async_copy(v_hbm.at[part], v_ref.at[part], load_sem.at[1, g]))
    for g in range(groups):
        part = pl.ds(g * GROUP, GROUP)
        loads.append(pltpu.make_async_copy(q_hbm.at[part], q_ref.at[part], load_sem.at[2, g]))
    for load in small + loads:
        load.start()

    small[0].wait()
    small[1].wait()
    anchor = me * rows
    start = [starts[d] for d in range(docs)]

    def last_start(position):
        last = start[0]
        for d in range(1, docs):
            last = jnp.where(start[d] <= position, start[d], last)
        return last

    def first_start(position):
        first = jnp.int32(2**30)
        for d in range(docs - 1, -1, -1):
            first = jnp.where(start[d] >= position, start[d], first)
        return first

    tail = last_start(anchor + rows - 1) - anchor
    row = lax.broadcasted_iota(jnp.int32, (GROUP, HD), 0)
    for g in range(groups):
        loads[2 * g].wait()
        loads[2 * g + 1].wait()
        part = pl.ds(g * GROUP, GROUP)
        keep = jnp.where(row + g * GROUP >= tail, 1.0, 0.0).astype(jnp.bfloat16)
        for h in range(head_count):
            lanes = pl.ds(h * HD, HD)
            add = lax.dot_general(
                k_ref[part, lanes] * keep,
                v_ref[part, lanes],
                (((0,), (0,)), ((), ())),
                preferred_element_type=jnp.float32,
            ).reshape(NZ, PIECE, HD)
            summ[:, h] = add if g == 0 else summ[:, h] + add

    pl.semaphore_wait(barrier, peers - 1 + teams - 1)
    for (dz, dx), t in zip(offsets(), owners):
        tz, tx = lax.rem(z + dz, NZ), lax.rem(x + dx, NX)
        send(summ.at[tz, tx], gath.at[me], ctx_send.at[0], ctx_recv.at[0], {"ctx": t})
    gath[me] = summ[z, x]

    for g in range(groups):
        loads[2 * groups + g].wait()
    state[...] = jnp.zeros_like(state)

    def local(c, _):
        r0 = pl.multiple_of(c * CHUNK, CHUNK)
        part = pl.ds(r0, CHUNK)
        base = anchor + r0
        position = base + lax.broadcasted_iota(jnp.int32, (CHUNK, HD), 0)
        source = base + lax.broadcasted_iota(jnp.int32, (CHUNK, CHUNK), 1)
        since = jnp.full((CHUNK, HD), start[0], jnp.int32)
        for d in range(1, docs):
            since = jnp.where(position >= start[d], start[d], since)
        allowed = jnp.where((source <= position) & (source >= since), 1.0, 0.0)
        allowed = jnp.concatenate([allowed, allowed], axis=1) > 0.0
        final = last_start(base + CHUNK - 1)
        live = jnp.where(position < first_start(base), 1.0, 0.0).astype(jnp.bfloat16)
        live = jnp.concatenate([live, live], axis=1)
        keep = jnp.where(position >= final, 1.0, 0.0).astype(jnp.bfloat16)
        keep = jnp.concatenate([keep, keep], axis=1)
        carry_on = jnp.where(final >= base, 0.0, 1.0)
        for p in range(head_count // 2):
            lanes = pl.ds(p * 2 * HD, 2 * HD)
            q, k, v = q_ref[part, lanes], k_ref[part, lanes], v_ref[part, lanes]
            scores = lax.dot_general(
                q, apart(k), (((1,), (1,)), ((), ())), preferred_element_type=jnp.float32
            )
            s_high, s_low = halves(jnp.where(allowed, scores, 0.0))
            before = state[p]
            b_high, b_low = halves(before)
            kept = k * keep
            turned = jnp.concatenate([kept[:, :HD].T, kept[:, HD:].T], axis=1)
            inner = dot(jnp.concatenate([s_high, s_low, turned], axis=0), apart(v))
            q_live = q * live
            across = dot(
                jnp.concatenate([q_live, q_live], axis=1),
                jnp.concatenate([apart(b_high), apart(b_low)], axis=0),
            )
            att[part, lanes] = inner[:CHUNK] + inner[CHUNK : 2 * CHUNK] + across
            state[p] = before * carry_on + inner[2 * CHUNK :]
        return 0

    lax.fori_loop(0, SPLIT, local, 0)

    slab = lax.broadcasted_iota(jnp.int32, (peers, HD), 0)
    since = jnp.full((peers, HD), start[0], jnp.int32)
    for d in range(1, docs):
        since = jnp.where((slab + 1) * rows - 1 >= start[d], start[d], since)
    going_on = jnp.where(since >= slab * rows, 0.0, 1.0)
    wait_bytes(gath.at[pl.ds(0, peers - 1)], ctx_recv.at[0])
    carry = jnp.zeros((PIECE, HD), jnp.float32)
    for m in range(peers):
        sums[m] = carry
        carry = carry * going_on[m : m + 1] + gath[m]
    for t in owners:
        send(sums.at[t], incoming.at[me], ctx_send.at[1], ctx_recv.at[1], {"ctx": t})
    incoming[me] = sums[me]

    lax.fori_loop(SPLIT, rows // CHUNK, local, 0)

    wait_bytes(incoming.at[pl.ds(0, peers - 1)], ctx_recv.at[1])
    entry = first_start(anchor) - anchor
    entering = []
    for p in range(head_count // 2):
        heads = []
        for h in (2 * p, 2 * p + 1):
            heads.append(jnp.concatenate([incoming[s * NX + h] for s in range(NZ)], axis=0))
        high, low = halves(jnp.concatenate(heads, axis=1))
        entering.append(jnp.concatenate([apart(high), apart(low)], axis=0))
    eye = lax.broadcasted_iota(jnp.int32, (128, 128), 0) == lax.broadcasted_iota(
        jnp.int32, (128, 128), 1
    )
    for g in range(groups):

        def finish(b, _, g=g):
            r0 = pl.multiple_of(g * GROUP + b * FINAL, FINAL)
            part = pl.ds(r0, FINAL)
            position = r0 + lax.broadcasted_iota(jnp.int32, (FINAL, HD), 0)
            live = jnp.where(position < entry, 1.0, 0.0).astype(jnp.bfloat16)
            live = jnp.concatenate([live, live], axis=1)
            total = jnp.zeros((FINAL, 2 * HD), jnp.float32)
            for p in range(head_count // 2):
                lanes = pl.ds(p * 2 * HD, 2 * HD)
                q = q_ref[part, lanes] * live
                a = att[part, lanes] + dot(jnp.concatenate([q, q], axis=1), entering[p])
                att[part, lanes] = a
                total = total + a * a
            total = total[:, :HD] + total[:, HD:]
            column = jnp.sum(total, axis=1, keepdims=True)
            for i in range(FINAL // 128):
                squares[g, pl.ds(b * (FINAL // 128) + i, 1)] = jnp.sum(
                    jnp.where(eye, column[i * 128 : i * 128 + 128], 0.0), axis=0, keepdims=True
                )
            return 0

        lax.fori_loop(0, GROUP // FINAL, finish, 0)
        for t in mates:
            send(
                squares.at[g], squares_in.at[g, team], head_send.at[g], head_recv.at[g], {"head": t}
            )
        squares_in[g, team] = squares[g]

    gain = gain_ref[...].astype(jnp.float32).reshape(1, head_count * HD)
    for g in range(groups):
        wait_bytes(squares_in.at[g, pl.ds(0, teams - 1)], head_recv.at[g])
        total = squares_in[g, 0]
        for m in range(1, teams):
            total = total + squares_in[g, m]
        scale = lax.rsqrt(total / (HEADS * HD) + 1e-06)
        for b in range(blocks):
            part = pl.ds(g * GROUP + b * 128, 128)
            column = jnp.sum(jnp.where(eye, scale[b : b + 1], 0.0), axis=1, keepdims=True)
            out_ref[part] = (att[part] * column * gain).astype(jnp.bfloat16)

    for side in range(2):
        wait_bytes((gath, incoming)[side].at[pl.ds(0, peers - 1)], ctx_send.at[side])
    for g in range(groups):
        wait_bytes(squares_in.at[g, pl.ds(0, teams - 1)], head_send.at[g])


def shards(query_rows, key_rows, value_rows, out_gain, doc_starts):
    rows, features = query_rows.shape
    head_count = features // HD
    groups = rows // GROUP
    peers = lax.axis_size("ctx")
    teams = lax.axis_size("head")
    hbm = pl.BlockSpec(memory_space=pltpu.HBM)
    vmem = pl.BlockSpec(memory_space=pltpu.VMEM)
    f32 = jnp.float32
    dma = pltpu.SemaphoreType.DMA
    operands = [
        pltpu.with_memory_space_constraint(array, pltpu.HBM)
        for array in (doc_starts, query_rows, key_rows, value_rows, out_gain)
    ]
    return pl.pallas_call(
        kernel,
        out_shape=jax.ShapeDtypeStruct((rows, features), jnp.bfloat16),
        in_specs=[hbm] * 5,
        out_specs=vmem,
        scratch_shapes=[
            pltpu.SMEM(doc_starts.shape, jnp.int32),
            pltpu.VMEM(out_gain.shape, jnp.bfloat16),
            pltpu.VMEM((rows, features), jnp.bfloat16),
            pltpu.VMEM((rows, features), jnp.bfloat16),
            pltpu.VMEM((rows, features), jnp.bfloat16),
            pltpu.VMEM((rows, features), f32),
            pltpu.VMEM((head_count // 2, HD, 2 * HD), f32),
            pltpu.VMEM((NZ, NX, PIECE, HD), f32),
            pltpu.VMEM((peers, PIECE, HD), f32),
            pltpu.VMEM((peers, PIECE, HD), f32),
            pltpu.VMEM((peers, PIECE, HD), f32),
            pltpu.VMEM((groups, GROUP // 128, 128), f32),
            pltpu.VMEM((groups, teams, GROUP // 128, 128), f32),
            dma((3, groups)),
            dma((2,)),
            dma((2,)),
            dma((2,)),
            dma((groups,)),
            dma((groups,)),
        ],
        compiler_params=pltpu.CompilerParams(
            collective_id=0, has_side_effects=True, vmem_limit_bytes=48 * 2**20
        ),
    )(*operands)


def solution(mesh):
    placed = (P("ctx", "head"), P("ctx", "head"), P("ctx", "head"), P("head"), P())
    return jax.shard_map(
        shards, mesh=mesh, in_specs=placed, out_specs=P("ctx", "head"), check_vma=False
    )
```
